32 devices in a mesh: grp: 1, row: 32 (over z, y, x, core), col: 1.
Axes of the slice: x: 2, y: 2, z: 4, core: 2. Of those that a mesh axis runs over, the one named last changes fastest.
Arguments:
- pair_map: bfloat16 [128, 128, 288], P(('grp', 'row'), 'col'), may hold values from -6 to 6
- norm_in: float32 [288], replicated, may hold values from 0.1 to 1.9
- w_query: bfloat16 [288, 256], replicated, may hold values from -12 to 12
- w_key: bfloat16 [288, 256], replicated, may hold values from -1 to 1
- w_value: bfloat16 [288, 256], replicated, may hold values from -0.375 to 0.375
- w_gate: bfloat16 [288, 256], replicated, may hold values from -0.375 to 0.375
- w_out: bfloat16 [256, 288], replicated, may hold values from -3 to 3
- norm_mid: float32 [288], replicated, may hold values from 0.1 to 1.9
- norm_out: float32 [288], replicated, may hold values from 0.1 to 1.9
- w_up: bfloat16 [288, 1152], replicated, may hold values from -0.375 to 0.375
- w_down: bfloat16 [1152, 288], replicated, may hold values from -0.1875 to 0.1875
Outputs:
- updated: bfloat16 [128, 128, 288], P(('grp', 'row'), 'col')
The draws below stay inside these ranges and needn't reach their ends.
All inputs are finite; a program needn't handle non-finite values.
Results may differ from the reference program's by a relative error of at most 0.014.
Values may be sent and summed in bfloat16 or wider, within the bound.
A program may use at most 64 MiB of HBM per device.

```python
import jax
import jax.numpy as jnp
from jax import lax

C = 288
HEADS = 8
HEAD_DIM = 32
FF = 1152
HD = 256
L = 128


def shared_base(key):
    return jax.random.truncated_normal(jax.random.fold_in(key, 7), -6.0, 6.0, (C, HD), jnp.float32) * C ** (-0.5)


def draw_w_key(key, part):
    return shared_base(key).astype(jnp.bfloat16)


def draw_w_query(key, part):
    independent = jax.random.truncated_normal(jax.random.fold_in(key, 11), -6.0, 6.0, (C, HD), jnp.float32) * C ** (-0.5)
    exponent = jax.random.uniform(jax.random.fold_in(key, 17), (HEADS,), jnp.float32, 0.0, jnp.log(2.5))
    temper = jnp.repeat(jnp.exp(exponent), HEAD_DIM)
    return (independent * temper[None, :]).astype(jnp.bfloat16)


def block_scale(own_key, extent, split, low, top_value):
    level, own = 1.0, jax.random.fold_in(own_key, 6)
    for position, shards_of in split:
        heights = jnp.exp(jax.random.uniform(jax.random.fold_in(own, position), (shards_of,), jnp.float32, low / len(split), top_value / len(split)))
        level = level * jnp.repeat(heights, extent[position] // shards_of).reshape([-1 if axis == position else 1 for axis in range(len(extent))])
    return level


def scatter_about(rng, extent, spread, limit, cuts=(), dtype=jnp.bfloat16):
    values = jax.random.normal(rng, extent, jnp.float32) * spread
    if len(cuts) > 0:
        values = block_scale(rng, extent, cuts, -0.22, 0.18) * values
    return jnp.clip(values, min=-limit, max=limit).astype(dtype)


def setup_inputs(seed: int = 0, part: int = 0) -> dict:
    seeds = jax.random.split(jax.random.key(seed), 12)
    part_splits = jax.random.split(jax.random.fold_in(seeds[11], part), 12)
    return {
        "pair_map": scatter_about(part_splits[0], (L, L, C), 1.0, 6.0, ((0, 32),)),
        "norm_in": jnp.clip(1.0 + 0.18 * jax.random.normal(seeds[1], (C,), jnp.float32), 0.1, 1.9),
        "w_query": draw_w_query(jax.random.fold_in(seeds[11], 71), part),
        "w_key": draw_w_key(jax.random.fold_in(seeds[11], 71), part),
        "w_value": scatter_about(seeds[4], (C, HD), C ** -0.5, 0.375),
        "w_gate": scatter_about(seeds[5], (C, HD), C ** -0.5, 0.375),
        "w_out": scatter_about(seeds[6], (HD, C), (max(HD // 64, 1)) ** -0.5, 3.0),
        "norm_mid": jnp.clip(1.0 + 0.18 * jax.random.normal(seeds[7], (C,), jnp.float32), 0.1, 1.9),
        "norm_out": jnp.clip(1.0 + 0.18 * jax.random.normal(seeds[8], (C,), jnp.float32), 0.1, 1.9),
        "w_up": scatter_about(seeds[9], (C, FF), C ** -0.5, 0.375),
        "w_down": scatter_about(seeds[10], (FF, C), FF ** -0.5, 0.1875),
    }


epsilon = 1e-06

def normalize(inputs, gain):
    mean_square = lax.optimization_barrier(jnp.mean(inputs * inputs, axis=-1, keepdims=True))
    return inputs * lax.rsqrt(mean_square + epsilon) * gain

def attend_rows(pair_rows, norm_in, w_query, w_key, w_value, w_gate, w_out, norm_mid):
    row_count = pair_rows.shape[0]
    length = pair_rows.shape[1]
    channels = pair_rows.shape[2]
    widened = pair_rows.astype(jnp.float32)
    normed = normalize(widened, norm_in).astype(jnp.bfloat16).reshape(row_count * length, channels)

    def project(weight):
        return jnp.dot(normed, weight, preferred_element_type=jnp.float32).astype(jnp.bfloat16)
    query_rows = project(w_query).reshape(row_count, length, HEADS, HEAD_DIM).transpose(2, 0, 1, 3)
    key_rows = project(w_key).reshape(row_count, length, HEADS, HEAD_DIM).transpose(2, 0, 1, 3)
    value_rows = project(w_value).reshape(row_count, length, HEADS, HEAD_DIM).transpose(2, 0, 1, 3)
    gate_rows = project(w_gate)
    score_scale = HEAD_DIM ** (-0.5)

    def one_head(triple):
        query_head, key_head, value_head = triple
        scores = jnp.einsum('mqd,mkd->mqk', query_head.astype(jnp.float32), key_head.astype(jnp.float32)) * score_scale
        scores = scores - lax.optimization_barrier(jnp.max(scores, axis=-1, keepdims=True))
        expanded = jnp.exp(scores)
        probabilities = (expanded / lax.optimization_barrier(jnp.sum(expanded, axis=-1, keepdims=True))).astype(jnp.bfloat16)
        return jnp.einsum('mqk,mkd->mqd', probabilities.astype(jnp.float32), value_head.astype(jnp.float32))
    head_outputs = lax.map(one_head, (query_rows, key_rows, value_rows))
    merged = head_outputs.transpose(1, 2, 0, 3).reshape(row_count * length, HEADS * HEAD_DIM)
    gated = (merged * jax.nn.sigmoid(gate_rows.astype(jnp.float32))).astype(jnp.bfloat16)
    update = jnp.dot(gated, w_out, preferred_element_type=jnp.float32).reshape(row_count, length, channels)
    return normalize(widened + update, norm_mid).astype(jnp.bfloat16)

def feed_forward(sym_rows, norm_out, w_up, w_down):
    shape_in = sym_rows.shape
    flat = sym_rows.reshape(-1, shape_in[-1]).astype(jnp.float32)
    normed = normalize(flat, norm_out).astype(jnp.bfloat16)
    hidden = jnp.maximum(jnp.dot(normed, w_up, preferred_element_type=jnp.float32), 0.0).astype(jnp.bfloat16)
    result = flat + jnp.dot(hidden, w_down, preferred_element_type=jnp.float32)
    return result.astype(jnp.bfloat16).reshape(shape_in)

def reference(pair_map, norm_in, w_query, w_key, w_value, w_gate, w_out, norm_mid, norm_out, w_up, w_down):
    length = pair_map.shape[0]
    channels = pair_map.shape[2]
    blocks = pair_map.reshape(length // 8, 8, length, channels)
    attended = lax.map(lambda block_rows: attend_rows(block_rows, norm_in, w_query, w_key, w_value, w_gate, w_out, norm_mid), blocks)
    attended = attended.reshape(length, length, channels)
    mirrored = jnp.transpose(attended, (1, 0, 2))
    symmetric = ((attended.astype(jnp.float32) + mirrored.astype(jnp.float32)) * 0.5).astype(jnp.bfloat16)
    output = lax.map(lambda block_rows: feed_forward(block_rows, norm_out, w_up, w_down), symmetric.reshape(length // 8, 8, length, channels))
    return output.reshape(length, length, channels)
```

```python
import functools

import jax
import jax.numpy as jnp
from jax import lax
from jax.experimental import pallas as pl
from jax.experimental.pallas import tpu as pltpu
from jax.sharding import PartitionSpec as P

HEADS = 8
HEAD_DIM = 32


epsilon = 1e-06


def normalize(inputs, gain):
    mean_square = jnp.mean(inputs * inputs, axis=-1, keepdims=True)
    return inputs * lax.rsqrt(mean_square + epsilon) * gain


def contract(left, right, left_dim, right_dim):
    return lax.dot_general(
        left, right, (((left_dim,), (right_dim,)), ((), ())), preferred_element_type=jnp.float32
    )


def exchange_matrix(pairs, own_rows, length, outgoing):
    target = lax.broadcasted_iota(jnp.int32, (pairs, pairs), 0)
    source = lax.broadcasted_iota(jnp.int32, (pairs, pairs), 1)
    block = own_rows * own_rows
    if outgoing:
        device = target // block
        column = (target % block) // own_rows
        row = target % own_rows
        wanted = row * length + device * own_rows + column
    else:
        column = target // length
        device = (target % length) // own_rows
        row = target % own_rows
        wanted = device * block + column * own_rows + row
    return jnp.where(source == wanted, 1.0, 0.0).astype(jnp.bfloat16)


def attend_kernel(
    x_ref, norm_in, w_query, w_key, w_value, w_gate, w_out, norm_mid, own_ref, send_ref, merged_ref
):
    own_rows, length, channels = x_ref.shape
    pairs = own_rows * length
    widened = x_ref[...].reshape(pairs, channels).astype(jnp.float32)
    normed = normalize(widened, norm_in[...]).astype(jnp.bfloat16)
    queries = contract(w_query[...], normed, 0, 1).astype(jnp.bfloat16)
    keys = contract(w_key[...], normed, 0, 1).astype(jnp.bfloat16)
    values = contract(w_value[...], normed, 0, 1).astype(jnp.bfloat16)
    gates = jax.nn.sigmoid(contract(w_gate[...], normed, 0, 1))
    scale = HEAD_DIM ** (-0.5)
    for row in range(own_rows):
        span = slice(row * length, (row + 1) * length)
        for head in range(HEADS):
            part = slice(head * HEAD_DIM, (head + 1) * HEAD_DIM)
            scores = contract(keys[part, span], queries[part, span], 0, 0)
            expanded = jnp.exp((scores - jnp.max(scores, axis=0, keepdims=True)) * scale)
            total = jnp.sum(expanded, axis=0, keepdims=True)
            attended = contract(values[part, span], expanded.astype(jnp.bfloat16), 1, 0)
            merged_ref[part, span] = (attended * (1.0 / total) * gates[part, span]).astype(
                jnp.bfloat16
            )
    update = contract(merged_ref[...], w_out[...], 0, 0)
    rowwise = normalize(widened + update, norm_mid[...]).astype(jnp.bfloat16)
    own_ref[...] = rowwise
    send_ref[...] = contract(
        exchange_matrix(pairs, own_rows, length, True), rowwise, 1, 0
    ).astype(jnp.bfloat16)


def transition_kernel(own_rows, length, own_ref, arrived_ref, norm_out, w_up, w_down, out_ref):
    pairs = own_rows * length
    mirrored = contract(exchange_matrix(pairs, own_rows, length, False), arrived_ref[...], 1, 0)
    symmetric = ((own_ref[...].astype(jnp.float32) + mirrored) * 0.5).astype(jnp.bfloat16)
    flat = symmetric.astype(jnp.float32)
    normed = normalize(flat, norm_out[...]).astype(jnp.bfloat16)
    hidden = jnp.maximum(contract(normed, w_up[...], 1, 0), 0.0).astype(jnp.bfloat16)
    out_ref[...] = (flat + contract(hidden, w_down[...], 1, 0)).astype(jnp.bfloat16)


def local(
    pair_map, norm_in, w_query, w_key, w_value, w_gate, w_out, norm_mid, norm_out, w_up, w_down
):
    col_count = lax.axis_size("col")
    row_count = lax.axis_size("row")
    tile_rows, tile_cols, channels = pair_map.shape
    own_rows = tile_rows // col_count
    length = tile_cols * col_count
    pairs = own_rows * length
    hidden = w_query.shape[1]
    rows = pair_map
    if col_count > 1:
        halves = pair_map.reshape(col_count, own_rows, tile_cols, channels)
        rows = lax.all_to_all(halves, "col", split_axis=0, concat_axis=2, tiled=True)[0]
    whole = pl.BlockSpec(memory_space=pltpu.VMEM)
    own, send = pl.pallas_call(
        attend_kernel,
        out_shape=[jax.ShapeDtypeStruct((pairs, channels), jnp.bfloat16)] * 2,
        in_specs=[whole] * 8,
        out_specs=[whole] * 2,
        scratch_shapes=[pltpu.VMEM((hidden, pairs), jnp.bfloat16)],
    )(rows, norm_in[None], w_query, w_key, w_value, w_gate, w_out, norm_mid[None])
    axes = ("row", "col") if col_count > 1 else "row"
    arrived = lax.all_to_all(
        send.reshape(row_count * col_count, own_rows * own_rows, channels),
        axes,
        split_axis=0,
        concat_axis=0,
        tiled=True,
    ).reshape(pairs, channels)
    finished = pl.pallas_call(
        functools.partial(transition_kernel, own_rows, length),
        out_shape=jax.ShapeDtypeStruct((pairs, channels), jnp.bfloat16),
        in_specs=[whole] * 5,
        out_specs=whole,
    )(own, arrived, norm_out[None], w_up, w_down)
    if col_count == 1:
        return finished.reshape(tile_rows, tile_cols, channels)
    returned = lax.all_to_all(
        finished.reshape(own_rows, col_count, tile_cols, channels),
        "col",
        split_axis=1,
        concat_axis=0,
        tiled=True,
    )
    return returned.reshape(tile_rows, tile_cols, channels)


def solution(mesh):
    placed = (P(("grp", "row"), "col", None), P(), P(), P(), P(), P(), P(), P(), P(), P(), P())
    return jax.shard_map(
        local, mesh=mesh, in_specs=placed, out_specs=P(("grp", "row"), "col", None), check_vma=False
    )
```

```python
import functools

import jax
import jax.numpy as jnp
from jax import lax
from jax.experimental import pallas as pl
from jax.experimental.pallas import tpu as pltpu
from jax.sharding import PartitionSpec as P

HEADS = 8
HEAD_DIM = 32
LANES = 128


epsilon = 1e-06


def normalize(inputs, gain):
    mean_square = jnp.mean(inputs * inputs, axis=0, keepdims=True)
    return inputs * lax.rsqrt(mean_square + epsilon) * gain


def contract(left, right, left_dim, right_dim):
    return lax.dot_general(
        left, right, (((left_dim,), (right_dim,)), ((), ())), preferred_element_type=jnp.float32
    )


def upright(gain, pairs):
    column = jnp.broadcast_to(gain, (LANES, gain.shape[1])).T
    return jnp.concatenate([column] * (pairs // LANES), axis=1)


def flatten(ref):
    return jnp.concatenate([ref[row] for row in range(ref.shape[0])], axis=1)


def outgoing(slots, padded, own_rows, length):
    shape = (slots, own_rows * length)
    slot = lax.broadcasted_iota(jnp.int32, shape, 0)
    pair = lax.broadcasted_iota(jnp.int32, shape, 1)
    within = slot % padded
    wanted = (within % own_rows) * length + (slot // padded) * own_rows + within // own_rows
    wanted = jnp.where(within < own_rows * own_rows, wanted, -1)
    return jnp.where(pair == wanted, 1.0, 0.0).astype(jnp.bfloat16)


def incoming(slots, padded, own_rows, length):
    shape = (slots, own_rows * length)
    slot = lax.broadcasted_iota(jnp.int32, shape, 0)
    pair = lax.broadcasted_iota(jnp.int32, shape, 1)
    device = (pair % length) // own_rows
    wanted = device * padded + (pair // length) * own_rows + pair % own_rows
    return jnp.where(slot == wanted, 1.0, 0.0).astype(jnp.bfloat16)


def attend_kernel(
    count,
    cols,
    x_ref,
    norm_in,
    w_query,
    w_key,
    w_value,
    w_gate,
    w_out,
    norm_mid,
    sym_ref,
    merged_ref,
    send_ref,
    land_ref,
    send_sem,
    recv_sem,
):
    own_rows, channels, length = x_ref.shape
    pairs = own_rows * length
    padded = send_ref.shape[1]
    me = lax.axis_index("row") * cols + lax.axis_index("col")

    def place(offset):
        other = lax.rem(me + offset, count)
        return {"row": other // cols, "col": lax.rem(other, cols)}

    def transfer(offset):
        other = lax.rem(me + offset, count)
        return pltpu.make_async_remote_copy(
            src_ref=send_ref.at[other],
            dst_ref=land_ref.at[me],
            send_sem=send_sem.at[offset],
            recv_sem=recv_sem.at[offset],
            device_id=place(offset),
            device_id_type=pl.DeviceIdType.MESH,
        )

    barrier = pltpu.get_barrier_semaphore()

    @pl.loop(1, count)
    def _(offset):
        pl.semaphore_signal(
            barrier, inc=1, device_id=place(offset), device_id_type=pl.DeviceIdType.MESH
        )

    widened = flatten(x_ref).astype(jnp.float32)
    normed = normalize(widened, upright(norm_in[...], pairs)).astype(jnp.bfloat16)
    queries = contract(w_query[...], normed, 0, 0).astype(jnp.bfloat16)
    keys = contract(w_key[...], normed, 0, 0).astype(jnp.bfloat16)
    values = contract(w_value[...], normed, 0, 0).astype(jnp.bfloat16)
    gates = jax.nn.sigmoid(contract(w_gate[...], normed, 0, 0))
    scale = HEAD_DIM ** (-0.5)
    for row in range(own_rows):
        span = slice(row * length, (row + 1) * length)
        for head in range(HEADS):
            part = slice(head * HEAD_DIM, (head + 1) * HEAD_DIM)
            scores = contract(keys[part, span], queries[part, span], 0, 0)
            expanded = jnp.exp((scores - jnp.max(scores, axis=0, keepdims=True)) * scale)
            total = jnp.sum(expanded, axis=0, keepdims=True)
            attended = contract(values[part, span], expanded.astype(jnp.bfloat16), 1, 0)
            merged_ref[part, span] = (attended * (1.0 / total) * gates[part, span]).astype(
                jnp.bfloat16
            )
    update = contract(w_out[...], merged_ref[...], 1, 0)
    rowwise = normalize(widened + update, upright(norm_mid[...], pairs)).astype(jnp.bfloat16)
    slots = count * padded
    send_ref[...] = (
        contract(outgoing(slots, padded, own_rows, length), rowwise, 1, 1)
        .astype(jnp.bfloat16)
        .reshape(count, padded, channels)
    )
    pl.semaphore_wait(barrier, count - 1)

    @pl.loop(1, count)
    def _(offset):
        transfer(offset).start()

    land_ref[me] = send_ref[me]
    arrange = incoming(slots, padded, own_rows, length)

    @pl.loop(1, count)
    def _(offset):
        transfer(offset).wait()

    mirrored = contract(land_ref[...].reshape(slots, channels), arrange, 0, 0)
    sym_ref[...] = ((rowwise.astype(jnp.float32) + mirrored) * 0.5).astype(jnp.bfloat16)


def transition_kernel(sym_ref, norm_out, w_up, w_down, out_ref):
    own_rows, channels, length = out_ref.shape
    flat = sym_ref[...].astype(jnp.float32)
    normed = normalize(flat, upright(norm_out[...], own_rows * length)).astype(jnp.bfloat16)
    hidden = jnp.maximum(contract(w_up[...], normed, 0, 0), 0.0).astype(jnp.bfloat16)
    result = (flat + contract(w_down[...], hidden, 1, 0)).astype(jnp.bfloat16)
    for row in range(own_rows):
        out_ref[row] = result[:, row * length : (row + 1) * length]


def local(
    pair_map, norm_in, w_query, w_key, w_value, w_gate, w_out, norm_mid, norm_out, w_up, w_down
):
    cols = lax.axis_size("col")
    count = lax.axis_size("row") * cols
    tile_rows, tile_cols, channels = pair_map.shape
    own_rows = tile_rows // cols
    length = tile_cols * cols
    pairs = own_rows * length
    padded = (own_rows * own_rows + 15) // 16 * 16
    rows = pair_map
    if cols > 1:
        halves = pair_map.reshape(cols, own_rows, tile_cols, channels)
        rows = lax.all_to_all(halves, "col", split_axis=0, concat_axis=2, tiled=True)[0]
    whole = pl.BlockSpec(memory_space=pltpu.VMEM)
    symmetric = pl.pallas_call(
        functools.partial(attend_kernel, count, cols),
        out_shape=jax.ShapeDtypeStruct((channels, pairs), jnp.bfloat16),
        in_specs=[whole] * 8,
        out_specs=whole,
        scratch_shapes=[
            pltpu.VMEM((w_query.shape[1], pairs), jnp.bfloat16),
            pltpu.VMEM((count, padded, channels), jnp.bfloat16),
            pltpu.VMEM((count, padded, channels), jnp.bfloat16),
            pltpu.SemaphoreType.DMA((count,)),
            pltpu.SemaphoreType.DMA((count,)),
        ],
        compiler_params=pltpu.CompilerParams(collective_id=0, has_side_effects=True),
    )(
        rows.transpose(0, 2, 1),
        norm_in[None],
        w_query,
        w_key,
        w_value,
        w_gate,
        w_out.T,
        norm_mid[None],
    )
    finished = pl.pallas_call(
        transition_kernel,
        out_shape=jax.ShapeDtypeStruct((own_rows, channels, length), jnp.bfloat16),
        in_specs=[whole] * 4,
        out_specs=whole,
    )(symmetric, norm_out[None], w_up, w_down.T).transpose(0, 2, 1)
    if cols == 1:
        return finished
    returned = lax.all_to_all(
        finished.reshape(own_rows, cols, tile_cols, channels),
        "col",
        split_axis=1,
        concat_axis=0,
        tiled=True,
    )
    return returned.reshape(tile_rows, tile_cols, channels)


def solution(mesh):
    placed = (P(("grp", "row"), "col", None), P(), P(), P(), P(), P(), P(), P(), P(), P(), P())
    return jax.shard_map(
        local, mesh=mesh, in_specs=placed, out_specs=P(("grp", "row"), "col", None), check_vma=False
    )
```

```python
import functools

import jax
import jax.numpy as jnp
from jax import lax
from jax.experimental import pallas as pl
from jax.experimental.pallas import tpu as pltpu
from jax.sharding import PartitionSpec as P

HEADS = 8
HEAD_DIM = 32
LANES = 128


epsilon = 1e-06


def normalize(inputs, gain):
    mean_square = jnp.mean(inputs * inputs, axis=0, keepdims=True)
    return inputs * lax.rsqrt(mean_square + epsilon) * gain


def contract(left, right, left_dim, right_dim):
    return lax.dot_general(
        left, right, (((left_dim,), (right_dim,)), ((), ())), preferred_element_type=jnp.float32
    )


def upright(gain, pairs):
    column = jnp.broadcast_to(gain[None], (LANES, gain.shape[0])).T
    return jnp.concatenate([column] * (pairs // LANES), axis=1)


def outgoing(slots, padded, phase_rows, own_rows, length):
    shape = (slots, phase_rows * length)
    slot = lax.broadcasted_iota(jnp.int32, shape, 0)
    pair = lax.broadcasted_iota(jnp.int32, shape, 1)
    within = slot % padded
    wanted = (within % phase_rows) * length + (slot // padded) * own_rows + within // phase_rows
    wanted = jnp.where(within < phase_rows * own_rows, wanted, -1)
    return jnp.where(pair == wanted, 1.0, 0.0).astype(jnp.bfloat16)


def incoming(phase, slots, padded, phase_rows, own_rows, length):
    shape = (slots, own_rows * length)
    slot = lax.broadcasted_iota(jnp.int32, shape, 0)
    pair = lax.broadcasted_iota(jnp.int32, shape, 1)
    device = (pair % length) // own_rows
    row = pair % own_rows
    wanted = device * padded + (pair // length) * phase_rows + row % phase_rows
    wanted = jnp.where(row // phase_rows == phase, wanted, -1)
    return jnp.where(slot == wanted, 1.0, 0.0).astype(jnp.bfloat16)


def attend_kernel(
    count,
    cols,
    x_ref,
    norm_in,
    w_query,
    w_key,
    w_value,
    w_gate,
    w_out,
    norm_mid,
    sym_ref,
    merged_ref,
    send_ref,
    land_ref,
    send_sem,
    recv_sem,
):
    own_rows, channels, length = x_ref.shape
    phases, _, padded, _ = send_ref.shape
    phase_rows = own_rows // phases
    phase_pairs = phase_rows * length
    slots = count * padded
    me = lax.axis_index("row") * cols + lax.axis_index("col")

    def place(offset):
        other = lax.rem(me + offset, count)
        return {"row": other // cols, "col": lax.rem(other, cols)}

    def transfer(phase, offset):
        other = lax.rem(me + offset, count)
        return pltpu.make_async_remote_copy(
            src_ref=send_ref.at[phase, other],
            dst_ref=land_ref.at[phase, me],
            send_sem=send_sem.at[phase, offset],
            recv_sem=recv_sem.at[phase, offset],
            device_id=place(offset),
            device_id_type=pl.DeviceIdType.MESH,
        )

    barrier = pltpu.get_barrier_semaphore()

    @pl.loop(1, count)
    def _(offset):
        pl.semaphore_signal(
            barrier, inc=1, device_id=place(offset), device_id_type=pl.DeviceIdType.MESH
        )

    gain_in = upright(norm_in[...], phase_pairs)
    gain_mid = upright(norm_mid[...], phase_pairs)
    ordering = outgoing(slots, padded, phase_rows, own_rows, length)
    scale = HEAD_DIM ** (-0.5)
    finished = []
    for phase in range(phases):
        rows = range(phase * phase_rows, (phase + 1) * phase_rows)
        widened = jnp.concatenate([x_ref[row] for row in rows], axis=1).astype(jnp.float32)
        normed = normalize(widened, gain_in).astype(jnp.bfloat16)
        queries = contract(w_query[...], normed, 0, 0).astype(jnp.bfloat16)
        keys = contract(w_key[...], normed, 0, 0).astype(jnp.bfloat16)
        values = contract(w_value[...], normed, 0, 0).astype(jnp.bfloat16)
        gates = jax.nn.sigmoid(contract(w_gate[...], normed, 0, 0))
        for row in range(phase_rows):
            span = slice(row * length, (row + 1) * length)
            for head in range(HEADS):
                part = slice(head * HEAD_DIM, (head + 1) * HEAD_DIM)
                scores = contract(keys[part, span], queries[part, span], 0, 0)
                expanded = jnp.exp((scores - jnp.max(scores, axis=0, keepdims=True)) * scale)
                total = jnp.sum(expanded, axis=0, keepdims=True)
                attended = contract(values[part, span], expanded.astype(jnp.bfloat16), 1, 0)
                merged_ref[phase, part, span] = (
                    attended * (1.0 / total) * gates[part, span]
                ).astype(jnp.bfloat16)
        update = contract(w_out[...], merged_ref[phase], 1, 0)
        rowwise = normalize(widened + update, gain_mid).astype(jnp.bfloat16)
        finished.append(rowwise)
        send_ref[phase] = (
            contract(ordering, rowwise, 1, 1)
            .reshape(count, padded, channels)
            .astype(jnp.bfloat16)
        )
        if phase == 0:
            pl.semaphore_wait(barrier, count - 1)

        @pl.loop(1, count)
        def _(offset, phase=phase):
            transfer(phase, offset).start()

        land_ref[phase, me] = send_ref[phase, me]

    total = jnp.concatenate(finished, axis=1).astype(jnp.float32)
    for phase in range(phases):
        arrange = incoming(phase, slots, padded, phase_rows, own_rows, length)

        @pl.loop(1, count)
        def _(offset, phase=phase):
            transfer(phase, offset).wait()

        landed = land_ref[phase].astype(jnp.float32).reshape(slots, channels)
        total += contract(landed.astype(jnp.bfloat16), arrange, 0, 0)
    sym_ref[...] = (total * 0.5).astype(jnp.bfloat16)


def transition_kernel(sym_ref, norm_out, w_up, w_down, out_ref):
    own_rows, channels, length = out_ref.shape
    flat = sym_ref[...].astype(jnp.float32)
    normed = normalize(flat, upright(norm_out[...], own_rows * length)).astype(jnp.bfloat16)
    hidden = jnp.maximum(contract(w_up[...], normed, 0, 0), 0.0).astype(jnp.bfloat16)
    result = (flat + contract(w_down[...], hidden, 1, 0)).astype(jnp.bfloat16)
    for row in range(own_rows):
        out_ref[row] = result[:, row * length : (row + 1) * length]


def local(
    pair_map, norm_in, w_query, w_key, w_value, w_gate, w_out, norm_mid, norm_out, w_up, w_down
):
    cols = lax.axis_size("col")
    count = lax.axis_size("row") * cols
    tile_rows, tile_cols, channels = pair_map.shape
    own_rows = tile_rows // cols
    length = tile_cols * cols
    pairs = own_rows * length
    phases = 2 if own_rows % 2 == 0 else 1
    padded = (own_rows // phases * own_rows + 7) // 8 * 8
    rows = pair_map
    if cols > 1:
        halves = pair_map.reshape(cols, own_rows, tile_cols, channels)
        rows = lax.all_to_all(halves, "col", split_axis=0, concat_axis=2, tiled=True)[0]
    whole = pl.BlockSpec(memory_space=pltpu.VMEM)
    symmetric = pl.pallas_call(
        functools.partial(attend_kernel, count, cols),
        out_shape=jax.ShapeDtypeStruct((channels, pairs), jnp.bfloat16),
        in_specs=[whole] * 8,
        out_specs=whole,
        scratch_shapes=[
            pltpu.VMEM((phases, w_query.shape[1], pairs // phases), jnp.bfloat16),
            pltpu.VMEM((phases, count, padded, channels), jnp.bfloat16),
            pltpu.VMEM((phases, count, padded, channels), jnp.bfloat16),
            pltpu.SemaphoreType.DMA((phases, count)),
            pltpu.SemaphoreType.DMA((phases, count)),
        ],
        compiler_params=pltpu.CompilerParams(collective_id=0, has_side_effects=True),
    )(
        rows.transpose(0, 2, 1),
        norm_in,
        w_query,
        w_key,
        w_value,
        w_gate,
        w_out.T,
        norm_mid,
    )
    finished = pl.pallas_call(
        transition_kernel,
        out_shape=jax.ShapeDtypeStruct((own_rows, channels, length), jnp.bfloat16),
        in_specs=[whole] * 4,
        out_specs=whole,
    )(symmetric, norm_out, w_up, w_down.T).transpose(0, 2, 1)
    if cols == 1:
        return finished
    returned = lax.all_to_all(
        finished.reshape(own_rows, cols, tile_cols, channels),
        "col",
        split_axis=1,
        concat_axis=0,
        tiled=True,
    )
    return returned.reshape(tile_rows, tile_cols, channels)


def solution(mesh):
    placed = (P(("grp", "row"), "col", None), P(), P(), P(), P(), P(), P(), P(), P(), P(), P())
    return jax.shard_map(
        local, mesh=mesh, in_specs=placed, out_specs=P(("grp", "row"), "col", None), check_vma=False
    )
```

```python
import functools

import jax
import jax.numpy as jnp
from jax import lax
from jax.experimental import pallas as pl
from jax.experimental.pallas import tpu as pltpu
from jax.sharding import PartitionSpec as P

HEADS = 8
HEAD_DIM = 32
LANES = 128


epsilon = 1e-06


def normalize(inputs, gain):
    mean_square = jnp.mean(inputs * inputs, axis=0, keepdims=True)
    return inputs * lax.rsqrt(mean_square + epsilon) * gain


def contract(left, right, left_dim, right_dim):
    return lax.dot_general(
        left, right, (((left_dim,), (right_dim,)), ((), ())), preferred_element_type=jnp.float32
    )


def upright(gain, pairs):
    column = jnp.broadcast_to(gain[None], (LANES, gain.shape[0])).T
    return jnp.concatenate([column] * (pairs // LANES), axis=1)


def outgoing(slots, padded, phase_rows, own_rows, length):
    shape = (slots, phase_rows * length)
    slot = lax.broadcasted_iota(jnp.int32, shape, 0)
    pair = lax.broadcasted_iota(jnp.int32, shape, 1)
    within = slot % padded
    wanted = (within % phase_rows) * length + (slot // padded) * own_rows + within // phase_rows
    wanted = jnp.where(within < phase_rows * own_rows, wanted, -1)
    return jnp.where(pair == wanted, 1.0, 0.0).astype(jnp.bfloat16)


def incoming(phase, slots, padded, phase_rows, own_rows, length):
    shape = (slots, own_rows * length)
    slot = lax.broadcasted_iota(jnp.int32, shape, 0)
    pair = lax.broadcasted_iota(jnp.int32, shape, 1)
    device = (pair % length) // own_rows
    row = pair % own_rows
    wanted = device * padded + (pair // length) * phase_rows + row % phase_rows
    wanted = jnp.where(row // phase_rows == phase, wanted, -1)
    return jnp.where(slot == wanted, 1.0, 0.0).astype(jnp.bfloat16)


def attend_kernel(
    count,
    cols,
    x_ref,
    norm_in,
    w_query,
    w_key,
    w_value,
    w_gate,
    w_out,
    norm_mid,
    sym_ref,
    merged_ref,
    send_ref,
    land_ref,
    send_sem,
    recv_sem,
):
    own_rows, channels, length = x_ref.shape
    phases, _, padded, _ = send_ref.shape
    phase_rows = own_rows // phases
    phase_pairs = phase_rows * length
    slots = count * padded
    me = lax.axis_index("row") * cols + lax.axis_index("col")

    def place(offset):
        other = lax.rem(me + offset, count)
        return {"row": other // cols, "col": lax.rem(other, cols)}

    def transfer(phase, offset):
        other = lax.rem(me + offset, count)
        return pltpu.make_async_remote_copy(
            src_ref=send_ref.at[phase, other],
            dst_ref=land_ref.at[phase, me],
            send_sem=send_sem.at[phase, offset],
            recv_sem=recv_sem.at[phase, offset],
            device_id=place(offset),
            device_id_type=pl.DeviceIdType.MESH,
        )

    barrier = pltpu.get_barrier_semaphore()

    @pl.loop(1, count)
    def _(offset):
        pl.semaphore_signal(
            barrier, inc=1, device_id=place(offset), device_id_type=pl.DeviceIdType.MESH
        )

    gain_in = upright(norm_in[...], phase_pairs)
    gain_mid = upright(norm_mid[...], phase_pairs)
    ordering = outgoing(slots, padded, phase_rows, own_rows, length)
    scale = HEAD_DIM ** (-0.5)
    finished = []
    for phase in range(phases):
        rows = range(phase * phase_rows, (phase + 1) * phase_rows)
        widened = jnp.concatenate([x_ref[row] for row in rows], axis=1).astype(jnp.float32)
        normed = normalize(widened, gain_in).astype(jnp.bfloat16)
        queries = contract(w_query[...], normed, 0, 0).astype(jnp.bfloat16)
        keys = contract(w_key[...], normed, 0, 0).astype(jnp.bfloat16)
        values = contract(w_value[...], normed, 0, 0).astype(jnp.bfloat16)
        gates = jax.nn.sigmoid(contract(w_gate[...], normed, 0, 0))
        for row in range(phase_rows):
            span = slice(row * length, (row + 1) * length)
            for head in range(HEADS):
                part = slice(head * HEAD_DIM, (head + 1) * HEAD_DIM)
                scores = contract(keys[part, span], queries[part, span], 0, 0)
                expanded = jnp.exp((scores - jnp.max(scores, axis=0, keepdims=True)) * scale)
                total = jnp.sum(expanded, axis=0, keepdims=True)
                attended = contract(values[part, span], expanded.astype(jnp.bfloat16), 1, 0)
                merged_ref[phase, part, span] = (
                    attended * (1.0 / total) * gates[part, span]
                ).astype(jnp.bfloat16)
        update = contract(w_out[...], merged_ref[phase], 1, 0)
        rowwise = normalize(widened + update, gain_mid).astype(jnp.bfloat16)
        finished.append(rowwise)
        send_ref[phase] = (
            contract(ordering, rowwise, 1, 1)
            .reshape(count, padded, channels)
            .astype(jnp.bfloat16)
        )
        if phase == 0:
            pl.semaphore_wait(barrier, count - 1)

        @pl.loop(1, count)
        def _(offset, phase=phase):
            transfer(phase, 1 + lax.rem(offset + count // 2, count - 1)).start()

        land_ref[phase, me] = send_ref[phase, me]

    total = jnp.concatenate(finished, axis=1).astype(jnp.float32)
    for phase in range(phases):
        arrange = incoming(phase, slots, padded, phase_rows, own_rows, length)

        @pl.loop(1, count)
        def _(offset, phase=phase):
            transfer(phase, offset).wait()

        landed = land_ref[phase].astype(jnp.float32).reshape(slots, channels)
        total += contract(landed.astype(jnp.bfloat16), arrange, 0, 0)
    sym_ref[...] = (total * 0.5).astype(jnp.bfloat16)


def transition_kernel(sym_ref, norm_out, w_up, w_down, out_ref):
    own_rows, channels, length = out_ref.shape
    flat = sym_ref[...].astype(jnp.float32)
    normed = normalize(flat, upright(norm_out[...], own_rows * length)).astype(jnp.bfloat16)
    hidden = jnp.maximum(contract(w_up[...], normed, 0, 0), 0.0).astype(jnp.bfloat16)
    result = (flat + contract(w_down[...], hidden, 1, 0)).astype(jnp.bfloat16)
    for row in range(own_rows):
        out_ref[row] = result[:, row * length : (row + 1) * length]


def local(
    pair_map, norm_in, w_query, w_key, w_value, w_gate, w_out, norm_mid, norm_out, w_up, w_down
):
    cols = lax.axis_size("col")
    count = lax.axis_size("row") * cols
    tile_rows, tile_cols, channels = pair_map.shape
    own_rows = tile_rows // cols
    length = tile_cols * cols
    pairs = own_rows * length
    phases = 2 if own_rows % 2 == 0 else 1
    padded = (own_rows // phases * own_rows + 7) // 8 * 8
    rows = pair_map
    if cols > 1:
        halves = pair_map.reshape(cols, own_rows, tile_cols, channels)
        rows = lax.all_to_all(halves, "col", split_axis=0, concat_axis=2, tiled=True)[0]
    whole = pl.BlockSpec(memory_space=pltpu.VMEM)
    symmetric = pl.pallas_call(
        functools.partial(attend_kernel, count, cols),
        out_shape=jax.ShapeDtypeStruct((channels, pairs), jnp.bfloat16),
        in_specs=[whole] * 8,
        out_specs=whole,
        scratch_shapes=[
            pltpu.VMEM((phases, w_query.shape[1], pairs // phases), jnp.bfloat16),
            pltpu.VMEM((phases, count, padded, channels), jnp.bfloat16),
            pltpu.VMEM((phases, count, padded, channels), jnp.bfloat16),
            pltpu.SemaphoreType.DMA((phases, count)),
            pltpu.SemaphoreType.DMA((phases, count)),
        ],
        compiler_params=pltpu.CompilerParams(collective_id=0, has_side_effects=True),
    )(
        rows.transpose(0, 2, 1),
        norm_in,
        w_query,
        w_key,
        w_value,
        w_gate,
        w_out.T,
        norm_mid,
    )
    finished = pl.pallas_call(
        transition_kernel,
        out_shape=jax.ShapeDtypeStruct((own_rows, channels, length), jnp.bfloat16),
        in_specs=[whole] * 4,
        out_specs=whole,
    )(symmetric, norm_out, w_up, w_down.T).transpose(0, 2, 1)
    if cols == 1:
        return finished
    returned = lax.all_to_all(
        finished.reshape(own_rows, cols, tile_cols, channels),
        "col",
        split_axis=1,
        concat_axis=0,
        tiled=True,
    )
    return returned.reshape(tile_rows, tile_cols, channels)


def solution(mesh):
    placed = (P(("grp", "row"), "col", None), P(), P(), P(), P(), P(), P(), P(), P(), P(), P())
    return jax.shard_map(
        local, mesh=mesh, in_specs=placed, out_specs=P(("grp", "row"), "col", None), check_vma=False
    )
```
